32 devices in a mesh: row: 8 (over z, y), col: 4 (over x, core).
Axes of the slice: x: 2, y: 2, z: 4, core: 2. Of those that a mesh axis runs over, the one named last changes fastest.
Arguments:
- object_tiles: float32 [2, 2, 3072, 1536], P(None, None, 'row', 'col'), may hold values from -4 to 4
- probe_field: float32 [2, 128, 128], replicated, may hold values from -4 to 4
- prop_phase: float32 [128, 128], replicated, may hold values from -3.140625 to 3.140625
- intensity: float32 [256, 128, 128], P(('row', 'col')), may hold values from 0 to 2
- positions: int32 [256, 2], P(('row', 'col')), may hold values from 0 to 383
- counts: int32 [8, 4], P('row'), may hold values from 1 to 8, as said below
Outputs:
- object_new: float32 [2, 2, 3072, 1536], P(None, None, 'row', 'col')
The draws below stay inside these ranges and needn't reach their ends.
Inputs may be any that keep to these rules, and one draw needn't show every extreme that they name: `counts`: in each row of the tile grid, in every aligned group of four tile columns 4j to 4j + 3, exactly two entries equal 8, and they sit at columns 4j and 4j + 1, or 4j + 2 and 4j + 3, or 4j and 4j + 2, or 4j + 1 and 4j + 3; the other two lie between 1 and 4.
All inputs are finite; a program needn't handle non-finite values.
Results may differ from the reference program's by a relative error of at most 0.0003.
Values sent between devices are 32-bit elements; how exact they have to be, the bound alone decides.
A program may use at most 64 MiB of HBM per device.

```python
import jax
import jax.numpy as jnp
from jax import lax

TILE = 384
FRAME = 128
FR_DEV = 8
ITERS = 2
KEEP = 4
OBJ_ROWS = 3072
OBJ_COLS = 1536
FRAMES = 256
N_ROW = 8
N_COL = 4


def draw_counts(key, part):
    pick_key = jax.random.fold_in(key, 11)
    light_key = jax.random.fold_in(key, 23)
    patterns = jnp.array([[1, 1, 0, 0], [0, 0, 1, 1], [1, 0, 1, 0], [0, 1, 0, 1]], dtype=jnp.int32)
    picks = jax.random.randint(pick_key, (N_ROW, N_COL // 4), 0, 4)
    busy_mask = patterns[picks].reshape(N_ROW, N_COL)
    light_load = jax.random.randint(light_key, (N_ROW, N_COL), 1, KEEP + 1)
    return jnp.where(busy_mask > 0, FR_DEV, light_load).astype(jnp.int32)


def with_ends(result, rng, low, largest):
    dims = result.shape
    index_at = [jax.random.randint(jax.random.fold_in(rng, axis), (), 0, dims[axis]) for axis in range(len(dims))]
    result = result.at[tuple(index_at)].set(low)
    longest = dims.index(max(dims))
    index_at[longest] = (index_at[longest] + 1) % dims[longest]
    return result.at[tuple(index_at)].set(largest)


def shard_levels(rng, dims, cuts, low, high):
    def one(position, parts):
        heights = jax.random.uniform(jax.random.fold_in(jax.random.fold_in(rng, 6), position), (parts,), jnp.float32, low / len(cuts), high / len(cuts))
        return jnp.repeat(jnp.exp(heights), dims[position] // parts).reshape((-1,) + (1,) * (len(dims) - position - 1))

    level = one(*cuts[0])
    for cut in cuts[1:]:
        level = level * one(*cut)
    return level


def normal_values(stream_key, extent, scale, limit, pieces=(), kind=jnp.bfloat16):
    drawn = jax.random.normal(stream_key, extent, jnp.float32) * scale
    if len(pieces) > 0:
        drawn = shard_levels(stream_key, extent, pieces, -0.22, 0.18) * drawn
    return jnp.clip(drawn, min=-limit, max=limit).astype(kind)


def setup_inputs(seed: int = 0) -> dict:
    keys = jax.random.split(jax.random.key(seed), 7)
    object_tiles = normal_values(keys[0], (2, 2, OBJ_ROWS, OBJ_COLS), 0.7, 4.0, ((2, 8), (3, 4)), jnp.float32)
    probe_field = normal_values(keys[1], (2, FRAME, FRAME), 0.7, 4.0, (), jnp.float32)
    prop_phase = jnp.clip(jax.random.uniform(keys[2], (FRAME, FRAME), jnp.float32, -3.140625, 3.140625), -3.140625, 3.140625)
    intensity = jnp.clip(2.0 * jax.random.uniform(keys[3], (FRAMES, FRAME, FRAME), jnp.float32) ** shard_levels(keys[3], (FRAMES, FRAME, FRAME), ((0, 32),), -0.2, 0.2), 0.0, 2.0)
    positions = with_ends(jax.random.randint(keys[4], (FRAMES, 2), 0, TILE), jax.random.fold_in(keys[4], 1), 0, TILE - 1).astype(jnp.int32)
    counts = draw_counts(jax.random.fold_in(keys[6], 71), 0)
    return dict(object_tiles=object_tiles, probe_field=probe_field, prop_phase=prop_phase, intensity=intensity, positions=positions, counts=counts)


step_size = 0.2


def frame_gradient(first_slice, second_slice, probe_wave, kernel, measured):
    lit_wave = probe_wave * first_slice
    inner_wave = jnp.fft.ifft2(kernel * jnp.fft.fft2(lit_wave, norm="ortho"), norm="ortho")
    far_field = jnp.fft.fft2(inner_wave * second_slice, norm="ortho")
    misfit = jnp.real(far_field) ** 2 + jnp.imag(far_field) ** 2 - measured
    back_field = jnp.fft.ifft2(misfit * far_field, norm="ortho")
    grad_second = jnp.conj(inner_wave) * back_field
    carried = jnp.fft.fft2(jnp.conj(second_slice) * back_field, norm="ortho")
    near_field = jnp.fft.ifft2(jnp.conj(kernel) * carried, norm="ortho")
    grad_first = jnp.conj(probe_wave) * near_field
    return jnp.stack([jnp.stack([jnp.real(grad_first), jnp.imag(grad_first)]),
                      jnp.stack([jnp.real(grad_second), jnp.imag(grad_second)])])


def reference(object_tiles, probe_field, prop_phase, intensity, positions, counts):
    padding = ((0, 0), (0, 0), (0, FRAME), (0, FRAME))
    padded = jnp.pad(object_tiles, padding)
    frame_ids = jnp.arange(FRAMES, dtype=jnp.int32)
    device_ids = frame_ids // FR_DEV
    grid_rows = device_ids // N_COL
    grid_cols = device_ids % N_COL
    active = ((frame_ids % FR_DEV) < counts[grid_rows, grid_cols]).astype(jnp.float32)
    top_rows = (grid_rows * TILE + positions[:, 0]).astype(jnp.int32)
    left_cols = (grid_cols * TILE + positions[:, 1]).astype(jnp.int32)
    probe_wave = lax.complex(probe_field[0], probe_field[1])
    kernel = lax.complex(jnp.cos(prop_phase), jnp.sin(prop_phase))
    for iteration in range(ITERS):
        source = padded

        def accumulate(grad_total, scan_item):
            top_row, left_col, weight, measured = scan_item
            corner_at = (jnp.int32(0), jnp.int32(0), top_row, left_col)
            patch_cut = lax.dynamic_slice(source, corner_at, (2, 2, FRAME, FRAME))
            first_slice = lax.complex(patch_cut[0, 0], patch_cut[0, 1])
            second_slice = lax.complex(patch_cut[1, 0], patch_cut[1, 1])
            gradient = frame_gradient(first_slice, second_slice, probe_wave, kernel, measured) * weight
            current = lax.dynamic_slice(grad_total, corner_at, (2, 2, FRAME, FRAME))
            return lax.dynamic_update_slice(grad_total, current + gradient, corner_at), None

        grad_total, unused = lax.scan(accumulate, jnp.zeros_like(source), (top_rows, left_cols, active, intensity))
        updated = source[:, :, :OBJ_ROWS, :OBJ_COLS] - step_size * grad_total[:, :, :OBJ_ROWS, :OBJ_COLS]
        padded = jnp.pad(updated, padding)
    return padded[:, :, :OBJ_ROWS, :OBJ_COLS]
```

```python
import functools

import jax
import jax.numpy as jnp
import numpy as np
from jax import lax
from jax.experimental import pallas as pl
from jax.experimental.pallas import tpu as pltpu
from jax.sharding import PartitionSpec as P

ITERS = 2
GROUP = 4
SUB = 8

step_size = 0.2


def dft_tables(size):
    index = np.arange(size)
    phase = (index[:, None] * index[None, :] % size) * (2.0 * np.pi / size)
    re = np.cos(phase) / np.sqrt(size)
    im = -np.sin(phase) / np.sqrt(size)
    rights, lefts = [], []
    for sign in (1.0, -1.0):
        right = np.block([[re, sign * im], [-sign * im, re]]).astype(np.float32)
        high = right.astype(jnp.bfloat16)
        low = (right - high.astype(np.float32)).astype(jnp.bfloat16)
        rights.append(np.concatenate([high, high, low], axis=0))
        lefts.append(np.concatenate([high.T, high.T, low.T], axis=1))
    return np.stack(rights), np.stack(lefts)


def split(x):
    high = x.astype(jnp.bfloat16)
    low = (x - high.astype(jnp.float32)).astype(jnp.bfloat16)
    return high, low


def by_right(waves, table):
    size = waves[0][0].shape[0]
    x = jnp.concatenate([jnp.concatenate(wave, axis=1) for wave in waves], axis=0)
    high, low = split(x)
    y = jnp.dot(
        jnp.concatenate([high, low, high], axis=1), table, preferred_element_type=jnp.float32
    )
    return [
        (y[i * size : (i + 1) * size, :size], y[i * size : (i + 1) * size, size:])
        for i in range(len(waves))
    ]


def by_left(waves, table):
    size = waves[0][0].shape[0]
    x = jnp.concatenate([jnp.concatenate(wave, axis=0) for wave in waves], axis=1)
    high, low = split(x)
    y = jnp.dot(
        table, jnp.concatenate([high, low, high], axis=0), preferred_element_type=jnp.float32
    )
    return [
        (y[:size, i * size : (i + 1) * size], y[size:, i * size : (i + 1) * size])
        for i in range(len(waves))
    ]


def mul(a, b):
    return (a[0] * b[0] - a[1] * b[1], a[0] * b[1] + a[1] * b[0])


def conj_mul(a, b):
    return (a[0] * b[0] + a[1] * b[1], a[0] * b[1] - a[1] * b[0])


def frames_kernel(
    counts_ref, pos_ref, main_hbm, right_hbm, below_hbm, corner_hbm, probe_ref, kern_ref,
    meas_ref, rtab_ref, ltab_ref, out_main, out_right, out_below, out_corner, ext, grad, sems,
):
    frame = probe_ref.shape[1]
    tile = main_hbm.shape[1]
    slots = meas_ref.shape[0]
    whole = tile + frame
    copies = [
        pltpu.make_async_copy(main_hbm, ext.at[:, pl.ds(0, tile), pl.ds(0, tile)], sems.at[0]),
        pltpu.make_async_copy(right_hbm, ext.at[:, pl.ds(0, tile), pl.ds(tile, frame)], sems.at[1]),
        pltpu.make_async_copy(below_hbm, ext.at[:, pl.ds(tile, frame), pl.ds(0, tile)], sems.at[2]),
        pltpu.make_async_copy(
            corner_hbm, ext.at[:, pl.ds(tile, frame), pl.ds(tile, frame)], sems.at[3]
        ),
    ]
    for copy in copies:
        copy.start()
    grad[...] = jnp.zeros_like(grad)
    for copy in copies:
        copy.wait()
    count = counts_ref[0]
    lane = lax.broadcasted_iota(jnp.int32, (frame + SUB, frame), 1)
    sub = lax.broadcasted_iota(jnp.int32, (frame // SUB + 1, SUB, frame), 1)
    edge = jnp.zeros((1, SUB, frame), jnp.float32)

    @pl.loop(0, (count + GROUP - 1) // GROUP)
    def _(group):
        places, firsts, seconds = [], [], []
        for i in range(GROUP):
            slot = group * GROUP + i
            here = jnp.minimum(slot, slots - 1)
            weight = (slot < count).astype(jnp.float32)
            top = pos_ref[2 * here]
            left = pos_ref[2 * here + 1]
            block = left // frame
            shift = left - block * frame
            near = pl.ds(pl.multiple_of(block * frame, frame), frame)
            far = pl.ds(pl.multiple_of(block * frame + frame, frame), frame)
            start = top // SUB * SUB
            drop = top - start
            rows = pl.ds(pl.multiple_of(start, SUB), frame + SUB)
            back = lax.rem(frame - shift, frame)
            lift = lax.rem(SUB - drop, SUB)
            planes = []
            for s in range(4):
                a = pltpu.roll(ext[s, rows, near], back, 1)
                b = pltpu.roll(ext[s, rows, far], back, 1)
                wide = jnp.where(lane < frame - shift, a, b).reshape(-1, SUB, frame)
                wide = pltpu.roll(wide, lift, 1)
                plane = jnp.where(sub[1:] < SUB - drop, wide[:-1], wide[1:])
                planes.append(plane.reshape(frame, frame))
            places.append((here, weight, rows, near, far, shift, drop))
            firsts.append((planes[0], planes[1]))
            seconds.append((planes[2], planes[3]))
        probe = (probe_ref[0], probe_ref[1])
        kern = (kern_ref[0], kern_ref[1])
        lit = [mul(probe, first) for first in firsts]
        freq = by_left(by_right(lit, rtab_ref[0]), ltab_ref[0])
        moved = [mul(kern, f) for f in freq]
        inner = by_right(by_left(moved, ltab_ref[1]), rtab_ref[1])
        leave = [mul(b, o) for b, o in zip(inner, seconds)]
        far_field = by_left(by_right(leave, rtab_ref[0]), ltab_ref[0])
        missed = []
        for place, (re, im) in zip(places, far_field):
            misfit = re * re + im * im - meas_ref[place[0]]
            missed.append((misfit * re, misfit * im))
        back_wave = by_right(by_left(missed, ltab_ref[1]), rtab_ref[1])
        grad_two = [conj_mul(b, g) for b, g in zip(inner, back_wave)]
        carry = [conj_mul(o, g) for o, g in zip(seconds, back_wave)]
        carried = by_left(by_right(carry, rtab_ref[0]), ltab_ref[0])
        unmoved = [conj_mul(kern, f) for f in carried]
        near_wave = by_right(by_left(unmoved, ltab_ref[1]), rtab_ref[1])
        grad_one = [conj_mul(probe, w) for w in near_wave]
        for place, one, two in zip(places, grad_one, grad_two):
            here, weight, rows, near, far, shift, drop = place
            for s, value in enumerate((one[0], one[1], two[0], two[1])):
                turned = pltpu.roll(value * weight, shift, 1).reshape(-1, SUB, frame)
                turned = pltpu.roll(turned, drop, 1)
                upper = jnp.concatenate([turned, edge], axis=0)
                lower = jnp.concatenate([edge, turned], axis=0)
                turned = jnp.where(sub >= drop, upper, lower).reshape(frame + SUB, frame)
                inside = lane >= shift
                grad[s, rows, near] += jnp.where(inside, turned, 0.0)
                grad[s, rows, far] += jnp.where(inside, 0.0, turned)

    outs = [
        pltpu.make_async_copy(grad.at[:, pl.ds(0, tile), pl.ds(0, tile)], out_main, sems.at[0]),
        pltpu.make_async_copy(grad.at[:, pl.ds(0, tile), pl.ds(tile, frame)], out_right, sems.at[1]),
        pltpu.make_async_copy(grad.at[:, pl.ds(tile, frame), pl.ds(0, tile)], out_below, sems.at[2]),
        pltpu.make_async_copy(
            grad.at[:, pl.ds(tile, frame), pl.ds(tile, frame)], out_corner, sems.at[3]
        ),
    ]
    for copy in outs:
        copy.start()
    for copy in outs:
        copy.wait()


def frame_grads(count, positions, main, right, below, corner, probe, kern, intensity, tables):
    frame = probe.shape[1]
    tile = main.shape[1]
    smem = pl.BlockSpec(memory_space=pltpu.SMEM)
    vmem = pl.BlockSpec(memory_space=pltpu.VMEM)
    anywhere = pl.BlockSpec(memory_space=pl.ANY)
    whole = tile + frame
    return pl.pallas_call(
        frames_kernel,
        out_shape=[
            jax.ShapeDtypeStruct((4, tile, tile), jnp.float32),
            jax.ShapeDtypeStruct((4, tile, frame), jnp.float32),
            jax.ShapeDtypeStruct((4, frame, tile), jnp.float32),
            jax.ShapeDtypeStruct((4, frame, frame), jnp.float32),
        ],
        in_specs=[smem, smem] + [anywhere] * 4 + [vmem] * 5,
        out_specs=[anywhere] * 4,
        scratch_shapes=[
            pltpu.VMEM((4, whole, whole), jnp.float32),
            pltpu.VMEM((4, whole, whole), jnp.float32),
            pltpu.SemaphoreType.DMA((4,)),
        ],
        compiler_params=pltpu.CompilerParams(vmem_limit_bytes=48 << 20),
    )(count, positions, main, right, below, corner, probe, kern, intensity, *tables)


def passed(x, by_row, by_col):
    rows, cols = lax.axis_size("row"), lax.axis_size("col")
    pairs = [
        (r * cols + c, (r + by_row) * cols + c + by_col)
        for r in range(rows)
        for c in range(cols)
        if 0 <= r + by_row < rows and 0 <= c + by_col < cols
    ]
    return lax.ppermute(x, ("row", "col"), pairs)


def local(object_tiles, probe_field, prop_phase, intensity, positions, counts):
    tile = object_tiles.shape[3]
    frame = probe_field.shape[1]
    tables = [jnp.asarray(t) for t in dft_tables(frame)]
    kern = jnp.stack([jnp.cos(prop_phase), jnp.sin(prop_phase)])
    count = lax.dynamic_slice(counts[0], (lax.axis_index("col"),), (1,))
    flat = positions.reshape(-1)
    current = object_tiles.reshape(4, tile, tile)
    for iteration in range(ITERS):
        right = passed(current[:, :, :frame], 0, -1)
        below = passed(current[:, :frame, :], -1, 0)
        corner = passed(current[:, :frame, :frame], -1, -1)
        g_main, g_right, g_below, g_corner = frame_grads(
            count, flat, current, right, below, corner, probe_field, kern, intensity, tables
        )
        g_right = passed(g_right, 0, 1)
        g_below = passed(g_below, 1, 0)
        g_corner = passed(g_corner, 1, 1)
        rest = tile - frame
        total = (
            g_main
            + jnp.pad(g_right, ((0, 0), (0, 0), (0, rest)))
            + jnp.pad(g_below, ((0, 0), (0, rest), (0, 0)))
            + jnp.pad(g_corner, ((0, 0), (0, rest), (0, rest)))
        )
        current = current - step_size * total
    return current.reshape(object_tiles.shape)


def solution(mesh):
    return jax.shard_map(
        local,
        mesh=mesh,
        in_specs=(
            P(None, None, "row", "col"),
            P(),
            P(),
            P(("row", "col"), None, None),
            P(("row", "col"), None),
            P("row", None),
        ),
        out_specs=P(None, None, "row", "col"),
        check_vma=False,
    )
```

```python
import functools

import jax
import jax.numpy as jnp
import numpy as np
from jax import lax
from jax.experimental import pallas as pl
from jax.experimental.pallas import tpu as pltpu
from jax.sharding import PartitionSpec as P

ITERS = 2
GROUP = 4
SUB = 8

step_size = 0.2


def dft_tables(size):
    index = np.arange(size)
    phase = (index[:, None] * index[None, :] % size) * (2.0 * np.pi / size)
    re = np.cos(phase) / np.sqrt(size)
    im = -np.sin(phase) / np.sqrt(size)
    rights, lefts = [], []
    for sign in (1.0, -1.0):
        right = np.block([[re, sign * im], [-sign * im, re]]).astype(np.float32)
        high = right.astype(jnp.bfloat16)
        low = (right - high.astype(np.float32)).astype(jnp.bfloat16)
        rights.append(np.concatenate([high, high, low], axis=0))
        lefts.append(np.concatenate([high.T, high.T, low.T], axis=1))
    return np.stack(rights), np.stack(lefts)


def split(x):
    high = x.astype(jnp.bfloat16)
    low = (x - high.astype(jnp.float32)).astype(jnp.bfloat16)
    return high, low


def by_right(waves, table):
    size = waves[0][0].shape[0]
    x = jnp.concatenate([jnp.concatenate(wave, axis=1) for wave in waves], axis=0)
    high, low = split(x)
    y = jnp.dot(
        jnp.concatenate([high, low, high], axis=1), table, preferred_element_type=jnp.float32
    )
    return [
        (y[i * size : (i + 1) * size, :size], y[i * size : (i + 1) * size, size:])
        for i in range(len(waves))
    ]


def by_left(waves, table):
    size = waves[0][0].shape[0]
    x = jnp.concatenate([jnp.concatenate(wave, axis=0) for wave in waves], axis=1)
    high, low = split(x)
    y = jnp.dot(
        table, jnp.concatenate([high, low, high], axis=0), preferred_element_type=jnp.float32
    )
    return [
        (y[:size, i * size : (i + 1) * size], y[size:, i * size : (i + 1) * size])
        for i in range(len(waves))
    ]


def mul(a, b):
    return (a[0] * b[0] - a[1] * b[1], a[0] * b[1] + a[1] * b[0])


def conj_mul(a, b):
    return (a[0] * b[0] + a[1] * b[1], a[0] * b[1] - a[1] * b[0])


def frames_kernel(
    counts_ref, pos_ref, main_hbm, right_hbm, below_hbm, corner_hbm, probe_ref, kern_ref,
    meas_ref, rtab_ref, ltab_ref, out_main, out_right, out_below, out_corner, ext, grad, sems,
):
    frame = probe_ref.shape[1]
    tile = main_hbm.shape[1]
    slots = meas_ref.shape[0]
    whole = tile + frame
    has_right = lax.axis_index("col") < lax.axis_size("col") - 1
    has_below = lax.axis_index("row") < lax.axis_size("row") - 1
    core, rim = pl.ds(0, tile), pl.ds(tile, frame)
    copies = [
        (pltpu.make_async_copy(main_hbm, ext.at[:, core, core], sems.at[0]), True, core, core),
        (pltpu.make_async_copy(right_hbm, ext.at[:, core, rim], sems.at[1]), has_right, core, rim),
        (pltpu.make_async_copy(below_hbm, ext.at[:, rim, core], sems.at[2]), has_below, rim, core),
        (
            pltpu.make_async_copy(corner_hbm, ext.at[:, rim, rim], sems.at[3]),
            has_right & has_below, rim, rim,
        ),
    ]
    for copy, there, rows, cols in copies:
        if there is True:
            copy.start()
            continue
        pl.when(there)(copy.start)

        @pl.when(jnp.logical_not(there))
        def _():
            part = ext.at[:, rows, cols]
            part[...] = jnp.zeros(part.shape, jnp.float32)

    grad[...] = jnp.zeros_like(grad)
    for copy, there, rows, cols in copies:
        if there is True:
            copy.wait()
        else:
            pl.when(there)(copy.wait)
    count = counts_ref[0]
    lane = lax.broadcasted_iota(jnp.int32, (frame + SUB, frame), 1)
    sub = lax.broadcasted_iota(jnp.int32, (frame // SUB + 1, SUB, frame), 1)
    edge = jnp.zeros((1, SUB, frame), jnp.float32)

    @pl.loop(0, (count + GROUP - 1) // GROUP)
    def _(group):
        places, firsts, seconds = [], [], []
        for i in range(GROUP):
            slot = group * GROUP + i
            here = jnp.minimum(slot, slots - 1)
            weight = (slot < count).astype(jnp.float32)
            top = pos_ref[2 * here]
            left = pos_ref[2 * here + 1]
            block = left // frame
            shift = left - block * frame
            near = pl.ds(pl.multiple_of(block * frame, frame), frame)
            far = pl.ds(pl.multiple_of(block * frame + frame, frame), frame)
            start = top // SUB * SUB
            drop = top - start
            rows = pl.ds(pl.multiple_of(start, SUB), frame + SUB)
            back = lax.rem(frame - shift, frame)
            lift = lax.rem(SUB - drop, SUB)
            planes = []
            for s in range(4):
                a = pltpu.roll(ext[s, rows, near], back, 1)
                b = pltpu.roll(ext[s, rows, far], back, 1)
                wide = jnp.where(lane < frame - shift, a, b).reshape(-1, SUB, frame)
                wide = pltpu.roll(wide, lift, 1)
                plane = jnp.where(sub[1:] < SUB - drop, wide[:-1], wide[1:])
                planes.append(plane.reshape(frame, frame))
            places.append((here, weight, rows, near, far, shift, drop))
            firsts.append((planes[0], planes[1]))
            seconds.append((planes[2], planes[3]))
        probe = (probe_ref[0], probe_ref[1])
        kern = (kern_ref[0], kern_ref[1])
        lit = [mul(probe, first) for first in firsts]
        freq = by_left(by_right(lit, rtab_ref[0]), ltab_ref[0])
        moved = [mul(kern, f) for f in freq]
        inner = by_right(by_left(moved, ltab_ref[1]), rtab_ref[1])
        leave = [mul(b, o) for b, o in zip(inner, seconds)]
        far_field = by_left(by_right(leave, rtab_ref[0]), ltab_ref[0])
        missed = []
        for place, (re, im) in zip(places, far_field):
            misfit = re * re + im * im - meas_ref[place[0]]
            missed.append((misfit * re, misfit * im))
        back_wave = by_right(by_left(missed, ltab_ref[1]), rtab_ref[1])
        grad_two = [conj_mul(b, g) for b, g in zip(inner, back_wave)]
        carry = [conj_mul(o, g) for o, g in zip(seconds, back_wave)]
        carried = by_left(by_right(carry, rtab_ref[0]), ltab_ref[0])
        unmoved = [conj_mul(kern, f) for f in carried]
        near_wave = by_right(by_left(unmoved, ltab_ref[1]), rtab_ref[1])
        grad_one = [conj_mul(probe, w) for w in near_wave]
        for place, one, two in zip(places, grad_one, grad_two):
            here, weight, rows, near, far, shift, drop = place
            for s, value in enumerate((one[0], one[1], two[0], two[1])):
                turned = pltpu.roll(value * weight, shift, 1).reshape(-1, SUB, frame)
                turned = pltpu.roll(turned, drop, 1)
                upper = jnp.concatenate([turned, edge], axis=0)
                lower = jnp.concatenate([edge, turned], axis=0)
                turned = jnp.where(sub >= drop, upper, lower).reshape(frame + SUB, frame)
                inside = lane >= shift
                grad[s, rows, near] += jnp.where(inside, turned, 0.0)
                grad[s, rows, far] += jnp.where(inside, 0.0, turned)

    outs = [
        pltpu.make_async_copy(grad.at[:, pl.ds(0, tile), pl.ds(0, tile)], out_main, sems.at[0]),
        pltpu.make_async_copy(grad.at[:, pl.ds(0, tile), pl.ds(tile, frame)], out_right, sems.at[1]),
        pltpu.make_async_copy(grad.at[:, pl.ds(tile, frame), pl.ds(0, tile)], out_below, sems.at[2]),
        pltpu.make_async_copy(
            grad.at[:, pl.ds(tile, frame), pl.ds(tile, frame)], out_corner, sems.at[3]
        ),
    ]
    for copy in outs:
        copy.start()
    for copy in outs:
        copy.wait()


def frame_grads(count, positions, main, right, below, corner, probe, kern, intensity, tables):
    frame = probe.shape[1]
    tile = main.shape[1]
    smem = pl.BlockSpec(memory_space=pltpu.SMEM)
    vmem = pl.BlockSpec(memory_space=pltpu.VMEM)
    anywhere = pl.BlockSpec(memory_space=pl.ANY)
    whole = tile + frame
    return pl.pallas_call(
        frames_kernel,
        out_shape=[
            jax.ShapeDtypeStruct((4, tile, tile), jnp.float32),
            jax.ShapeDtypeStruct((4, tile, frame), jnp.float32),
            jax.ShapeDtypeStruct((4, frame, tile), jnp.float32),
            jax.ShapeDtypeStruct((4, frame, frame), jnp.float32),
        ],
        in_specs=[smem, smem] + [anywhere] * 4 + [vmem] * 5,
        out_specs=[anywhere] * 4,
        scratch_shapes=[
            pltpu.VMEM((4, whole, whole), jnp.float32),
            pltpu.VMEM((4, whole, whole), jnp.float32),
            pltpu.SemaphoreType.DMA((4,)),
        ],
        compiler_params=pltpu.CompilerParams(vmem_limit_bytes=48 << 20),
    )(count, positions, main, right, below, corner, probe, kern, intensity, *tables)


MESH = pl.DeviceIdType.MESH


class Around:
    def __init__(self):
        rows, cols = lax.axis_size("row"), lax.axis_size("col")
        row, col = lax.axis_index("row"), lax.axis_index("col")
        self.up = (lax.rem(row + rows - 1, rows), col)
        self.down = (lax.rem(row + 1, rows), col)
        self.left = (row, lax.rem(col + cols - 1, cols))
        self.right = (row, lax.rem(col + 1, cols))
        self.has_up = row > 0
        self.has_down = row < rows - 1
        self.has_left = col > 0
        self.has_right = col < cols - 1

    def meet(self):
        barrier = pltpu.get_barrier_semaphore()
        sides = (
            (self.has_up, self.up),
            (self.has_down, self.down),
            (self.has_left, self.left),
            (self.has_right, self.right),
        )
        for there, device in sides:

            @pl.when(there)
            def _():
                pl.semaphore_signal(barrier, inc=1, device_id=device, device_id_type=MESH)

        total = sum(there.astype(jnp.int32) for there, _ in sides)
        pl.semaphore_wait(barrier, total)


class Sends:
    def __init__(self, send_sems, recv_sems):
        self.send_sems, self.recv_sems = send_sems, recv_sems
        self.copies = {}

    def add(self, number, src, dst, device, has_target, has_source):
        copy = pltpu.make_async_remote_copy(
            src_ref=src,
            dst_ref=dst,
            send_sem=self.send_sems.at[number],
            recv_sem=self.recv_sems.at[number],
            device_id=device,
            device_id_type=MESH,
        )
        self.copies[number] = (copy, has_target, has_source)

    def start(self, number):
        copy, has_target, _ = self.copies[number]
        pl.when(has_target)(copy.start)

    def arrived(self, number):
        copy, _, has_source = self.copies[number]
        pl.when(has_source)(copy.wait_recv)

    def drain(self):
        for copy, has_target, _ in self.copies.values():
            pl.when(has_target)(copy.wait_send)


def extend_kernel(main, right_out, below_out, corner_out, send_sems, recv_sems):
    tile = main.shape[2]
    frame = right_out.shape[2]
    chunks = tile // frame
    around = Around()
    sends = Sends(send_sems, recv_sems)
    for j in range(chunks):
        part = pl.ds(j * frame, frame)
        sends.add(
            j, main.at[:, pl.ds(0, frame), part], below_out.at[:, :, part], around.up,
            around.has_up, around.has_down,
        )
    sends.add(
        chunks, main.at[:, :, pl.ds(0, frame)], right_out, around.left,
        around.has_left, around.has_right,
    )
    sends.add(
        chunks + 1, below_out.at[:, :, pl.ds(0, frame)], corner_out, around.left,
        around.has_left & around.has_down, around.has_right & around.has_down,
    )
    around.meet()
    for number in range(chunks + 1):
        sends.start(number)
    sends.arrived(0)
    sends.start(chunks + 1)
    for number in range(1, chunks + 2):
        sends.arrived(number)
    sends.drain()


def fold_kernel(extend, main, g_main, g_right, g_below, g_corner, new, *rest):
    if extend:
        right_out, below_out, corner_out, *rest = rest
    obj, own, head, low, in_right, in_below, in_corner, send_sems, recv_sems, sems = rest
    tile = main.shape[2]
    frame = g_corner.shape[2]
    chunks = tile // frame
    first, after = pl.ds(0, frame), pl.ds(frame, tile - frame)
    parts = [pl.ds(j * frame, frame) for j in range(chunks)]
    around = Around()
    sends = Sends(send_sems, recv_sems)
    corner_number, right_number, below_number = 0, 1, 2
    sends.add(corner_number, g_corner, in_corner, around.right, around.has_right, around.has_left)
    sends.add(right_number, g_right, in_right, around.right, around.has_right, around.has_left)
    for j, part in enumerate(parts):
        src = low if j == 0 else g_below.at[:, :, part]
        sends.add(
            below_number + j, src, in_below.at[:, :, part], around.down,
            around.has_down, around.has_up,
        )
    rim_number = below_number + chunks
    side_number = rim_number + chunks
    if extend:
        for j, part in enumerate(parts):
            sends.add(
                rim_number + j, new.at[:, first, part], below_out.at[:, :, part], around.up,
                around.has_up, around.has_down,
            )
        for j, part in enumerate((first, after)):
            sends.add(
                side_number + j, new.at[:, part, first], right_out.at[:, part, :], around.left,
                around.has_left, around.has_right,
            )
        sends.add(
            side_number + 2, below_out.at[:, :, first], corner_out, around.left,
            around.has_left & around.has_down, around.has_right & around.has_down,
        )
    loads = [
        pltpu.make_async_copy(g_below.at[:, :, first], head, sems.at[0]),
        pltpu.make_async_copy(main, obj, sems.at[1]),
        pltpu.make_async_copy(g_main, own, sems.at[2]),
    ]
    for load in loads:
        load.start()

    @pl.when(jnp.logical_not(around.has_left))
    def _():
        in_right[...] = jnp.zeros_like(in_right)
        in_corner[...] = jnp.zeros_like(in_corner)

    @pl.when(jnp.logical_not(around.has_up))
    def _():
        in_below[...] = jnp.zeros_like(in_below)

    around.meet()
    sends.start(corner_number)
    sends.start(right_number)
    for j in range(1, chunks):
        sends.start(below_number + j)
    loads[0].wait()
    sends.arrived(corner_number)
    low[...] = head[...] + in_corner[...]
    sends.start(below_number)
    loads[1].wait()
    loads[2].wait()
    new[:, after, after] = obj[:, after, after] - step_size * own[:, after, after]
    sends.arrived(right_number)
    new[:, after, first] = obj[:, after, first] - step_size * (
        own[:, after, first] + in_right[:, after, :]
    )
    if extend:
        sends.start(side_number + 1)
    order = [1, 0] + list(range(2, chunks)) if chunks > 1 else [0]
    for j in order:
        part = parts[j]
        sends.arrived(below_number + j)
        total = own[:, first, part] + in_below[:, :, part]
        if j == 0:
            total = total + in_right[:, first, :]
        new[:, first, part] = obj[:, first, part] - step_size * total
        if extend:
            sends.start(rim_number + j)
            if j == 0:
                sends.start(side_number)
    if extend:
        sends.arrived(rim_number)
        sends.start(side_number + 2)
        for j in range(1, chunks):
            sends.arrived(rim_number + j)
        for number in range(side_number, side_number + 3):
            sends.arrived(number)
    sends.drain()


def extend_call(main, frame):
    tile = main.shape[2]
    anywhere = pl.BlockSpec(memory_space=pl.ANY)
    copies = tile // frame + 2
    return pl.pallas_call(
        extend_kernel,
        out_shape=rim_shapes(tile, frame),
        in_specs=[anywhere],
        out_specs=[anywhere] * 3,
        scratch_shapes=[pltpu.SemaphoreType.DMA((copies,)), pltpu.SemaphoreType.DMA((copies,))],
        compiler_params=pltpu.CompilerParams(collective_id=0, has_side_effects=True),
    )(main)


def rim_shapes(tile, frame):
    shapes = ((4, tile, frame), (4, frame, tile), (4, frame, frame))
    return [jax.ShapeDtypeStruct(shape, jnp.float32) for shape in shapes]


def fold_call(main, grads, extend):
    tile = main.shape[2]
    frame = grads[3].shape[2]
    anywhere = pl.BlockSpec(memory_space=pl.ANY)
    vmem = pl.BlockSpec(memory_space=pltpu.VMEM)
    copies = 2 * (tile // frame) + 5
    outs = [jax.ShapeDtypeStruct(main.shape, jnp.float32)]
    block = pltpu.VMEM((4, frame, frame), jnp.float32)
    return pl.pallas_call(
        functools.partial(fold_kernel, extend),
        out_shape=outs + (rim_shapes(tile, frame) if extend else []),
        in_specs=[anywhere] * 5,
        out_specs=[vmem] + ([anywhere] * 3 if extend else []),
        scratch_shapes=[
            pltpu.VMEM(main.shape, jnp.float32),
            pltpu.VMEM(main.shape, jnp.float32),
            block,
            block,
            pltpu.VMEM((4, tile, frame), jnp.float32),
            pltpu.VMEM((4, frame, tile), jnp.float32),
            block,
            pltpu.SemaphoreType.DMA((copies,)),
            pltpu.SemaphoreType.DMA((copies,)),
            pltpu.SemaphoreType.DMA((3,)),
        ],
        compiler_params=pltpu.CompilerParams(
            collective_id=1 if extend else 2, has_side_effects=True, vmem_limit_bytes=32 << 20
        ),
    )(main, *grads)


def local(object_tiles, probe_field, prop_phase, intensity, positions, counts):
    tile = object_tiles.shape[3]
    frame = probe_field.shape[1]
    tables = [jnp.asarray(t) for t in dft_tables(frame)]
    kern = jnp.stack([jnp.cos(prop_phase), jnp.sin(prop_phase)])
    count = lax.dynamic_slice(counts[0], (lax.axis_index("col"),), (1,))
    flat = positions.reshape(-1)
    current = object_tiles.reshape(4, tile, tile)
    rims = extend_call(current, frame)
    for iteration in range(ITERS):
        grads = frame_grads(count, flat, current, *rims, probe_field, kern, intensity, tables)
        current, *rims = fold_call(current, grads, iteration < ITERS - 1)
    return current.reshape(object_tiles.shape)


def solution(mesh):
    return jax.shard_map(
        local,
        mesh=mesh,
        in_specs=(
            P(None, None, "row", "col"),
            P(),
            P(),
            P(("row", "col"), None, None),
            P(("row", "col"), None),
            P("row", None),
        ),
        out_specs=P(None, None, "row", "col"),
        check_vma=False,
    )
```

```python
import functools

import jax
import jax.numpy as jnp
import numpy as np
from jax import lax
from jax.experimental import pallas as pl
from jax.experimental.pallas import tpu as pltpu
from jax.sharding import PartitionSpec as P

ITERS = 2
GROUP = 4
SUB = 8

step_size = 0.2


def dft_tables(size):
    index = np.arange(size)
    phase = (index[:, None] * index[None, :] % size) * (2.0 * np.pi / size)
    re = np.cos(phase) / np.sqrt(size)
    im = -np.sin(phase) / np.sqrt(size)
    rights, lefts = [], []
    for sign in (1.0, -1.0):
        right = np.block([[re, sign * im], [-sign * im, re]]).astype(np.float32)
        high = right.astype(jnp.bfloat16)
        low = (right - high.astype(np.float32)).astype(jnp.bfloat16)
        rights.append(np.concatenate([high, high, low], axis=0))
        lefts.append(np.concatenate([high.T, high.T, low.T], axis=1))
    return np.stack(rights), np.stack(lefts)


def split(x):
    high = x.astype(jnp.bfloat16)
    low = (x - high.astype(jnp.float32)).astype(jnp.bfloat16)
    return high, low


def by_right(waves, table):
    size = waves[0][0].shape[0]
    x = jnp.concatenate([jnp.concatenate(wave, axis=1) for wave in waves], axis=0)
    high, low = split(x)
    y = jnp.dot(
        jnp.concatenate([high, low, high], axis=1), table, preferred_element_type=jnp.float32
    )
    return [
        (y[i * size : (i + 1) * size, :size], y[i * size : (i + 1) * size, size:])
        for i in range(len(waves))
    ]


def by_left(waves, table):
    size = waves[0][0].shape[0]
    x = jnp.concatenate([jnp.concatenate(wave, axis=0) for wave in waves], axis=1)
    high, low = split(x)
    y = jnp.dot(
        table, jnp.concatenate([high, low, high], axis=0), preferred_element_type=jnp.float32
    )
    return [
        (y[:size, i * size : (i + 1) * size], y[size:, i * size : (i + 1) * size])
        for i in range(len(waves))
    ]


def mul(a, b):
    return (a[0] * b[0] - a[1] * b[1], a[0] * b[1] + a[1] * b[0])


def conj_mul(a, b):
    return (a[0] * b[0] + a[1] * b[1], a[0] * b[1] - a[1] * b[0])


def frames_kernel(
    counts_ref, pos_ref, ext, probe_ref, kern_ref, meas_ref, rtab_ref, ltab_ref, grad,
):
    frame = probe_ref.shape[1]
    slots = meas_ref.shape[0]
    grad[...] = jnp.zeros_like(grad)
    count = counts_ref[0, lax.axis_index("col")]
    lane = lax.broadcasted_iota(jnp.int32, (frame + SUB, frame), 1)
    sub = lax.broadcasted_iota(jnp.int32, (frame // SUB + 1, SUB, frame), 1)
    edge = jnp.zeros((1, SUB, frame), jnp.float32)

    @pl.loop(0, (count + GROUP - 1) // GROUP)
    def _(group):
        places, firsts, seconds = [], [], []
        for i in range(GROUP):
            slot = group * GROUP + i
            here = jnp.minimum(slot, slots - 1)
            weight = (slot < count).astype(jnp.float32)
            top = pos_ref[here, 0]
            left = pos_ref[here, 1]
            block = left // frame
            shift = left - block * frame
            near = pl.ds(pl.multiple_of(block * frame, frame), frame)
            far = pl.ds(pl.multiple_of(block * frame + frame, frame), frame)
            start = top // SUB * SUB
            drop = top - start
            rows = pl.ds(pl.multiple_of(start, SUB), frame + SUB)
            back = lax.rem(frame - shift, frame)
            lift = lax.rem(SUB - drop, SUB)
            planes = []
            for s in range(4):
                a = pltpu.roll(ext[s, rows, near], back, 1)
                b = pltpu.roll(ext[s, rows, far], back, 1)
                wide = jnp.where(lane < frame - shift, a, b).reshape(-1, SUB, frame)
                wide = pltpu.roll(wide, lift, 1)
                plane = jnp.where(sub[1:] < SUB - drop, wide[:-1], wide[1:])
                planes.append(plane.reshape(frame, frame))
            places.append((here, weight, rows, near, far, shift, drop))
            firsts.append((planes[0], planes[1]))
            seconds.append((planes[2], planes[3]))
        probe = (probe_ref[0], probe_ref[1])
        kern = (kern_ref[0], kern_ref[1])
        lit = [mul(probe, first) for first in firsts]
        freq = by_left(by_right(lit, rtab_ref[0]), ltab_ref[0])
        moved = [mul(kern, f) for f in freq]
        inner = by_right(by_left(moved, ltab_ref[1]), rtab_ref[1])
        leave = [mul(b, o) for b, o in zip(inner, seconds)]
        far_field = by_left(by_right(leave, rtab_ref[0]), ltab_ref[0])
        missed = []
        for place, (re, im) in zip(places, far_field):
            misfit = re * re + im * im - meas_ref[place[0]]
            missed.append((misfit * re, misfit * im))
        back_wave = by_right(by_left(missed, ltab_ref[1]), rtab_ref[1])
        grad_two = [conj_mul(b, g) for b, g in zip(inner, back_wave)]
        carry = [conj_mul(o, g) for o, g in zip(seconds, back_wave)]
        carried = by_left(by_right(carry, rtab_ref[0]), ltab_ref[0])
        unmoved = [conj_mul(kern, f) for f in carried]
        near_wave = by_right(by_left(unmoved, ltab_ref[1]), rtab_ref[1])
        grad_one = [conj_mul(probe, w) for w in near_wave]
        for place, one, two in zip(places, grad_one, grad_two):
            here, weight, rows, near, far, shift, drop = place
            for s, value in enumerate((one[0], one[1], two[0], two[1])):
                turned = pltpu.roll(value * weight, shift, 1).reshape(-1, SUB, frame)
                turned = pltpu.roll(turned, drop, 1)
                upper = jnp.concatenate([turned, edge], axis=0)
                lower = jnp.concatenate([edge, turned], axis=0)
                turned = jnp.where(sub >= drop, upper, lower).reshape(frame + SUB, frame)
                inside = lane >= shift
                grad[s, rows, near] += jnp.where(inside, turned, 0.0)
                grad[s, rows, far] += jnp.where(inside, 0.0, turned)


def frame_grads(counts, positions, ext, probe, kern, intensity, tables):
    smem = pl.BlockSpec(memory_space=pltpu.SMEM)
    vmem = pl.BlockSpec(memory_space=pltpu.VMEM)
    return pl.pallas_call(
        frames_kernel,
        out_shape=jax.ShapeDtypeStruct(ext.shape, jnp.float32),
        in_specs=[smem, smem] + [vmem] * 6,
        out_specs=vmem,
        compiler_params=pltpu.CompilerParams(vmem_limit_bytes=40 << 20),
    )(counts, positions, ext, probe, kern, intensity, *tables)


MESH = pl.DeviceIdType.MESH


class Around:
    def __init__(self):
        rows, cols = lax.axis_size("row"), lax.axis_size("col")
        row, col = lax.axis_index("row"), lax.axis_index("col")
        self.up = (lax.rem(row + rows - 1, rows), col)
        self.down = (lax.rem(row + 1, rows), col)
        self.left = (row, lax.rem(col + cols - 1, cols))
        self.right = (row, lax.rem(col + 1, cols))
        self.has_up = row > 0
        self.has_down = row < rows - 1
        self.has_left = col > 0
        self.has_right = col < cols - 1

    def meet(self):
        barrier = pltpu.get_barrier_semaphore()
        sides = (
            (self.has_up, self.up),
            (self.has_down, self.down),
            (self.has_left, self.left),
            (self.has_right, self.right),
        )
        for there, device in sides:

            @pl.when(there)
            def _():
                pl.semaphore_signal(barrier, inc=1, device_id=device, device_id_type=MESH)

        total = sum(there.astype(jnp.int32) for there, _ in sides)
        pl.semaphore_wait(barrier, total)


class Sends:
    def __init__(self, send_sems, recv_sems):
        self.send_sems, self.recv_sems = send_sems, recv_sems
        self.copies = {}

    def add(self, number, src, dst, device, has_target, has_source):
        copy = pltpu.make_async_remote_copy(
            src_ref=src,
            dst_ref=dst,
            send_sem=self.send_sems.at[number],
            recv_sem=self.recv_sems.at[number],
            device_id=device,
            device_id_type=MESH,
        )
        self.copies[number] = (copy, has_target, has_source)

    def start(self, number):
        copy, has_target, _ = self.copies[number]
        pl.when(has_target)(copy.start)

    def arrived(self, number):
        copy, _, has_source = self.copies[number]
        pl.when(has_source)(copy.wait_recv)

    def drain(self):
        for copy, has_target, _ in self.copies.values():
            pl.when(has_target)(copy.wait_send)


def extend_kernel(main, phase, ext, kern, send_sems, recv_sems, sem):
    tile = main.shape[2]
    frame = phase.shape[0]
    chunks = tile // frame
    core, rim, first = pl.ds(0, tile), pl.ds(tile, frame), pl.ds(0, frame)
    around = Around()
    sends = Sends(send_sems, recv_sems)
    for j in range(chunks):
        part = pl.ds(j * frame, frame)
        sends.add(
            j, main.at[:, first, part], ext.at[:, rim, part], around.up,
            around.has_up, around.has_down,
        )
    sends.add(
        chunks, main.at[:, :, first], ext.at[:, core, rim], around.left,
        around.has_left, around.has_right,
    )
    sends.add(
        chunks + 1, ext.at[:, rim, first], ext.at[:, rim, rim], around.left,
        around.has_left & around.has_down, around.has_right & around.has_down,
    )
    around.meet()
    for number in range(chunks + 1):
        sends.start(number)
    load = pltpu.make_async_copy(main, ext.at[:, core, core], sem)
    load.start()
    kern[0] = jnp.cos(phase[...])
    kern[1] = jnp.sin(phase[...])
    clear_edges(around, ext, tile, frame)
    sends.arrived(0)
    sends.start(chunks + 1)
    load.wait()
    for number in range(1, chunks + 2):
        sends.arrived(number)
    sends.drain()


def clear_edges(around, ext, tile, frame):
    @pl.when(jnp.logical_not(around.has_right))
    def _():
        ext[:, :tile, tile:] = jnp.zeros((4, tile, frame), jnp.float32)

    @pl.when(jnp.logical_not(around.has_down))
    def _():
        ext[:, tile:, :tile] = jnp.zeros((4, frame, tile), jnp.float32)

    @pl.when(jnp.logical_not(around.has_right & around.has_down))
    def _():
        ext[:, tile:, tile:] = jnp.zeros((4, frame, frame), jnp.float32)


def fold_kernel(extend, tile, frame, ext, grad, new, *rest):
    if extend:
        in_top, high, *rest = rest
    low, in_right, in_below, in_corner, send_sems, recv_sems = rest
    chunks = tile // frame
    core, rim = pl.ds(0, tile), pl.ds(tile, frame)
    first, after = pl.ds(0, frame), pl.ds(frame, tile - frame)
    parts = [pl.ds(j * frame, frame) for j in range(chunks)]
    around = Around()
    sends = Sends(send_sems, recv_sems)
    corner_no, side_no, below_no = 0, 1, 3
    top_no = below_no + chunks
    rim_no = top_no + chunks
    there, source = around.has_right, around.has_left
    sends.add(corner_no, grad.at[:, rim, rim], in_corner, around.right, there, source)
    for j, part in enumerate((first, after)):
        sends.add(
            side_no + j, grad.at[:, part, rim], in_right.at[:, part, :], around.right, there, source
        )
    for j, part in enumerate(parts):
        sends.add(
            below_no + j, low if j == 0 else grad.at[:, rim, part], in_below.at[:, :, part],
            around.down, around.has_down, around.has_up,
        )
        if extend:
            sends.add(
                top_no + j, high if j == 0 else grad.at[:, first, part], in_top.at[:, :, part],
                around.up, around.has_up, around.has_down,
            )
    if extend:
        for j, part in enumerate((first, after)):
            sends.add(
                rim_no + j, new.at[:, part, first], new.at[:, part, rim], around.left,
                around.has_left, around.has_right,
            )
        sends.add(
            rim_no + 2, new.at[:, rim, first], new.at[:, rim, rim], around.left,
            around.has_left & around.has_down, around.has_right & around.has_down,
        )

    around.meet()

    def start_row(j):
        sends.start(below_no + j)
        if extend:
            sends.start(top_no + j)

    sends.start(corner_no)
    sends.start(side_no)
    if chunks > 1:
        start_row(1)
        sends.start(side_no + 1)

    @pl.when(jnp.logical_not(around.has_left))
    def _():
        in_right[...] = jnp.zeros_like(in_right)
        in_corner[...] = jnp.zeros_like(in_corner)

    @pl.when(jnp.logical_not(around.has_up))
    def _():
        in_below[...] = jnp.zeros_like(in_below)

    if extend:
        clear_edges(around, new, tile, frame)
    sends.arrived(corner_no)
    low[...] = grad[:, rim, first] + in_corner[...]
    sends.start(below_no)
    sends.arrived(side_no)
    if extend:
        high[...] = grad[:, first, first] + in_right[:, first, :]
        sends.start(top_no)
    for j in range(2, chunks):
        start_row(j)
    new[:, after, after] = ext[:, after, after] - step_size * grad[:, after, after]
    if chunks > 1:
        sends.arrived(side_no + 1)
        new[:, after, first] = ext[:, after, first] - step_size * (
            grad[:, after, first] + in_right[:, after, :]
        )
        if extend:
            sends.start(rim_no + 1)
    order = [1, 0] + list(range(2, chunks)) if chunks > 1 else [0]
    for j in order:
        part = parts[j]
        sends.arrived(below_no + j)
        total = grad[:, first, part] + in_below[:, :, part]
        if j == 0:
            total = total + in_right[:, first, :]
        new[:, first, part] = ext[:, first, part] - step_size * total
        if extend:
            if j == 0:
                sends.start(rim_no)
            sends.arrived(top_no + j)

            @pl.when(around.has_down)
            def _():
                own = low[...] if j == 0 else grad[:, rim, part]
                new[:, rim, part] = ext[:, rim, part] - step_size * (own + in_top[:, :, part])

            if j == 0:
                sends.start(rim_no + 2)
    if extend:
        for number in range(rim_no, rim_no + 3):
            if chunks > 1 or number != rim_no + 1:
                sends.arrived(number)
    sends.drain()


def extend_call(main, phase):
    tile, frame = main.shape[2], phase.shape[0]
    anywhere = pl.BlockSpec(memory_space=pl.ANY)
    vmem = pl.BlockSpec(memory_space=pltpu.VMEM)
    copies = tile // frame + 2
    whole = tile + frame
    return pl.pallas_call(
        extend_kernel,
        out_shape=[
            jax.ShapeDtypeStruct((4, whole, whole), jnp.float32),
            jax.ShapeDtypeStruct((2, frame, frame), jnp.float32),
        ],
        in_specs=[anywhere, vmem],
        out_specs=[vmem] * 2,
        scratch_shapes=[
            pltpu.SemaphoreType.DMA((copies,)),
            pltpu.SemaphoreType.DMA((copies,)),
            pltpu.SemaphoreType.DMA,
        ],
        compiler_params=pltpu.CompilerParams(
            collective_id=0, has_side_effects=True, vmem_limit_bytes=16 << 20
        ),
    )(main, phase)


def fold_call(ext, grad, frame, extend):
    whole = ext.shape[2]
    tile = whole - frame
    vmem = pl.BlockSpec(memory_space=pltpu.VMEM)
    copies = 2 * (tile // frame) + 6
    side = whole if extend else tile
    block = pltpu.VMEM((4, frame, frame), jnp.float32)
    strip = pltpu.VMEM((4, frame, tile), jnp.float32)
    return pl.pallas_call(
        functools.partial(fold_kernel, extend, tile, frame),
        out_shape=jax.ShapeDtypeStruct((4, side, side), jnp.float32),
        in_specs=[vmem] * 2,
        out_specs=vmem,
        scratch_shapes=([strip, block] if extend else [])
        + [
            block,
            pltpu.VMEM((4, tile, frame), jnp.float32),
            strip,
            block,
            pltpu.SemaphoreType.DMA((copies,)),
            pltpu.SemaphoreType.DMA((copies,)),
        ],
        compiler_params=pltpu.CompilerParams(
            collective_id=1 if extend else 2, has_side_effects=True, vmem_limit_bytes=32 << 20
        ),
    )(ext, grad)


def local(object_tiles, probe_field, prop_phase, intensity, positions, counts):
    tile = object_tiles.shape[3]
    frame = probe_field.shape[1]
    tables = [jnp.asarray(t) for t in dft_tables(frame)]
    ext, kern = extend_call(object_tiles.reshape(4, tile, tile), prop_phase)
    for iteration in range(ITERS):
        grad = frame_grads(counts, positions, ext, probe_field, kern, intensity, tables)
        ext = fold_call(ext, grad, frame, iteration < ITERS - 1)
    return ext.reshape(object_tiles.shape)


def solution(mesh):
    return jax.shard_map(
        local,
        mesh=mesh,
        in_specs=(
            P(None, None, "row", "col"),
            P(),
            P(),
            P(("row", "col"), None, None),
            P(("row", "col"), None),
            P("row", None),
        ),
        out_specs=P(None, None, "row", "col"),
        check_vma=False,
    )
```

```python
import functools

import jax
import jax.numpy as jnp
import numpy as np
from jax import lax
from jax.experimental import pallas as pl
from jax.experimental.pallas import tpu as pltpu
from jax.sharding import PartitionSpec as P

ITERS = 2
GROUP = 8
CHAIN = 2
SUB = 8

step_size = 0.2


def dft_tables(size):
    index = np.arange(size)
    phase = (index[:, None] * index[None, :] % size) * (2.0 * np.pi / size)
    re = np.cos(phase) / np.sqrt(size)
    im = -np.sin(phase) / np.sqrt(size)
    rights, lefts = [], []
    for sign in (1.0, -1.0):
        right = np.block([[re, sign * im], [-sign * im, re]]).astype(np.float32)
        high = right.astype(jnp.bfloat16)
        low = (right - high.astype(np.float32)).astype(jnp.bfloat16)
        rights.append(np.concatenate([high, high, low], axis=0))
        lefts.append(np.concatenate([high.T, high.T, low.T], axis=1))
    return np.stack(rights), np.stack(lefts)


def split(x):
    high = x.astype(jnp.bfloat16)
    low = (x - high.astype(jnp.float32)).astype(jnp.bfloat16)
    return high, low


def in_chains(transform):
    def over_all(waves, table):
        out = []
        for i in range(0, len(waves), CHAIN):
            out += transform(waves[i : i + CHAIN], table)
        return out

    return over_all


@in_chains
def by_right(waves, table):
    size = waves[0][0].shape[0]
    x = jnp.concatenate([jnp.concatenate(wave, axis=1) for wave in waves], axis=0)
    high, low = split(x)
    y = jnp.dot(
        jnp.concatenate([high, low, high], axis=1), table, preferred_element_type=jnp.float32
    )
    return [
        (y[i * size : (i + 1) * size, :size], y[i * size : (i + 1) * size, size:])
        for i in range(len(waves))
    ]


@in_chains
def by_left(waves, table):
    size = waves[0][0].shape[0]
    x = jnp.concatenate([jnp.concatenate(wave, axis=0) for wave in waves], axis=1)
    high, low = split(x)
    y = jnp.dot(
        table, jnp.concatenate([high, low, high], axis=0), preferred_element_type=jnp.float32
    )
    return [
        (y[:size, i * size : (i + 1) * size], y[size:, i * size : (i + 1) * size])
        for i in range(len(waves))
    ]


def mul(a, b):
    return (a[0] * b[0] - a[1] * b[1], a[0] * b[1] + a[1] * b[0])


def conj_mul(a, b):
    return (a[0] * b[0] + a[1] * b[1], a[0] * b[1] - a[1] * b[0])


def frames_kernel(
    counts_ref, pos_ref, ext, probe_ref, kern_ref, meas_ref, rtab_ref, ltab_ref, grad,
):
    frame = probe_ref.shape[1]
    slots = meas_ref.shape[0]
    grad[...] = jnp.zeros_like(grad)
    count = counts_ref[0, lax.axis_index("col")]
    lane = lax.broadcasted_iota(jnp.int32, (frame + SUB, frame), 1)
    sub = lax.broadcasted_iota(jnp.int32, (frame // SUB + 1, SUB, frame), 1)
    edge = jnp.zeros((1, SUB, frame), jnp.float32)

    @pl.loop(0, (count + GROUP - 1) // GROUP)
    def _(group):
        places, firsts, seconds = [], [], []
        for i in range(GROUP):
            slot = group * GROUP + i
            here = jnp.minimum(slot, slots - 1)
            weight = (slot < count).astype(jnp.float32)
            top = pos_ref[here, 0]
            left = pos_ref[here, 1]
            block = left // frame
            shift = left - block * frame
            near = pl.ds(pl.multiple_of(block * frame, frame), frame)
            far = pl.ds(pl.multiple_of(block * frame + frame, frame), frame)
            start = top // SUB * SUB
            drop = top - start
            rows = pl.ds(pl.multiple_of(start, SUB), frame + SUB)
            back = lax.rem(frame - shift, frame)
            lift = lax.rem(SUB - drop, SUB)
            planes = []
            for s in range(4):
                a = pltpu.roll(ext[s, rows, near], back, 1)
                b = pltpu.roll(ext[s, rows, far], back, 1)
                wide = jnp.where(lane < frame - shift, a, b).reshape(-1, SUB, frame)
                wide = pltpu.roll(wide, lift, 1)
                plane = jnp.where(sub[1:] < SUB - drop, wide[:-1], wide[1:])
                planes.append(plane.reshape(frame, frame))
            places.append((here, weight, rows, near, far, shift, drop))
            firsts.append((planes[0], planes[1]))
            seconds.append((planes[2], planes[3]))
        probe = (probe_ref[0], probe_ref[1])
        kern = (kern_ref[0], kern_ref[1])
        lit = [mul(probe, first) for first in firsts]
        freq = by_left(by_right(lit, rtab_ref[0]), ltab_ref[0])
        moved = [mul(kern, f) for f in freq]
        inner = by_right(by_left(moved, ltab_ref[1]), rtab_ref[1])
        leave = [mul(b, o) for b, o in zip(inner, seconds)]
        far_field = by_left(by_right(leave, rtab_ref[0]), ltab_ref[0])
        missed = []
        for place, (re, im) in zip(places, far_field):
            misfit = re * re + im * im - meas_ref[place[0]]
            missed.append((misfit * re, misfit * im))
        back_wave = by_right(by_left(missed, ltab_ref[1]), rtab_ref[1])
        grad_two = [conj_mul(b, g) for b, g in zip(inner, back_wave)]
        carry = [conj_mul(o, g) for o, g in zip(seconds, back_wave)]
        carried = by_left(by_right(carry, rtab_ref[0]), ltab_ref[0])
        unmoved = [conj_mul(kern, f) for f in carried]
        near_wave = by_right(by_left(unmoved, ltab_ref[1]), rtab_ref[1])
        grad_one = [conj_mul(probe, w) for w in near_wave]
        for place, one, two in zip(places, grad_one, grad_two):
            here, weight, rows, near, far, shift, drop = place
            for s, value in enumerate((one[0], one[1], two[0], two[1])):
                turned = pltpu.roll(value * weight, shift, 1).reshape(-1, SUB, frame)
                turned = pltpu.roll(turned, drop, 1)
                upper = jnp.concatenate([turned, edge], axis=0)
                lower = jnp.concatenate([edge, turned], axis=0)
                turned = jnp.where(sub >= drop, upper, lower).reshape(frame + SUB, frame)
                inside = lane >= shift
                grad[s, rows, near] += jnp.where(inside, turned, 0.0)
                grad[s, rows, far] += jnp.where(inside, 0.0, turned)


def frame_grads(counts, positions, ext, probe, kern, intensity, tables):
    smem = pl.BlockSpec(memory_space=pltpu.SMEM)
    vmem = pl.BlockSpec(memory_space=pltpu.VMEM)
    return pl.pallas_call(
        frames_kernel,
        out_shape=jax.ShapeDtypeStruct(ext.shape, jnp.float32),
        in_specs=[smem, smem] + [vmem] * 6,
        out_specs=vmem,
        compiler_params=pltpu.CompilerParams(vmem_limit_bytes=40 << 20),
    )(counts, positions, ext, probe, kern, intensity, *tables)


MESH = pl.DeviceIdType.MESH


class Around:
    def __init__(self):
        rows, cols = lax.axis_size("row"), lax.axis_size("col")
        row, col = lax.axis_index("row"), lax.axis_index("col")
        self.up = (lax.rem(row + rows - 1, rows), col)
        self.down = (lax.rem(row + 1, rows), col)
        self.left = (row, lax.rem(col + cols - 1, cols))
        self.right = (row, lax.rem(col + 1, cols))
        self.has_up = row > 0
        self.has_down = row < rows - 1
        self.has_left = col > 0
        self.has_right = col < cols - 1

    def meet(self):
        barrier = pltpu.get_barrier_semaphore()
        sides = (
            (self.has_up, self.up),
            (self.has_down, self.down),
            (self.has_left, self.left),
            (self.has_right, self.right),
        )
        for there, device in sides:

            @pl.when(there)
            def _():
                pl.semaphore_signal(barrier, inc=1, device_id=device, device_id_type=MESH)

        total = sum(there.astype(jnp.int32) for there, _ in sides)
        pl.semaphore_wait(barrier, total)


class Sends:
    def __init__(self, send_sems, recv_sems):
        self.send_sems, self.recv_sems = send_sems, recv_sems
        self.copies = {}

    def add(self, number, src, dst, device, has_target, has_source):
        copy = pltpu.make_async_remote_copy(
            src_ref=src,
            dst_ref=dst,
            send_sem=self.send_sems.at[number],
            recv_sem=self.recv_sems.at[number],
            device_id=device,
            device_id_type=MESH,
        )
        self.copies[number] = (copy, has_target, has_source)

    def start(self, number):
        copy, has_target, _ = self.copies[number]
        pl.when(has_target)(copy.start)

    def arrived(self, number):
        copy, _, has_source = self.copies[number]
        pl.when(has_source)(copy.wait_recv)

    def drain(self):
        for copy, has_target, _ in self.copies.values():
            pl.when(has_target)(copy.wait_send)


def extend_kernel(held, main, phase_hbm, *rest):
    later, (ext, kern), near = rest[:held], rest[held : held + 2], rest[held + 2 : 2 * held + 2]
    phase, send_sems, recv_sems, sems = rest[2 * held + 2 :]
    tile = main.shape[2]
    frame = phase.shape[0]
    chunks = tile // frame
    core, rim, first = pl.ds(0, tile), pl.ds(tile, frame), pl.ds(0, frame)
    around = Around()
    sends = Sends(send_sems, recv_sems)
    for j in range(chunks):
        part = pl.ds(j * frame, frame)
        sends.add(
            j, main.at[:, first, part], ext.at[:, rim, part], around.up,
            around.has_up, around.has_down,
        )
    sends.add(
        chunks, main.at[:, :, first], ext.at[:, core, rim], around.left,
        around.has_left, around.has_right,
    )
    sends.add(
        chunks + 1, ext.at[:, rim, first], ext.at[:, rim, rim], around.left,
        around.has_left & around.has_down, around.has_right & around.has_down,
    )
    around.meet()
    for number in range(chunks + 1):
        sends.start(number)
    phase_load = pltpu.make_async_copy(phase_hbm, phase, sems.at[0])
    loads = [pltpu.make_async_copy(main, ext.at[:, core, core], sems.at[1])] + [
        pltpu.make_async_copy(src, dst, sems.at[2 + i]) for i, (src, dst) in enumerate(zip(later, near))
    ]
    phase_load.start()
    for load in loads:
        load.start()
    phase_load.wait()
    kern[0] = jnp.cos(phase[...])
    kern[1] = jnp.sin(phase[...])
    clear_edges(around, ext, tile, frame)
    sends.arrived(0)
    sends.start(chunks + 1)
    for load in loads:
        load.wait()
    for number in range(1, chunks + 2):
        sends.arrived(number)
    sends.drain()


def clear_edges(around, ext, tile, frame):
    @pl.when(jnp.logical_not(around.has_right))
    def _():
        ext[:, :tile, tile:] = jnp.zeros((4, tile, frame), jnp.float32)

    @pl.when(jnp.logical_not(around.has_down))
    def _():
        ext[:, tile:, :tile] = jnp.zeros((4, frame, tile), jnp.float32)

    @pl.when(jnp.logical_not(around.has_right & around.has_down))
    def _():
        ext[:, tile:, tile:] = jnp.zeros((4, frame, frame), jnp.float32)


def fold_kernel(extend, tile, frame, ext, grad, new, *rest):
    if extend:
        in_top, high, *rest = rest
    low, in_right, in_below, in_corner, send_sems, recv_sems = rest
    chunks = tile // frame
    core, rim = pl.ds(0, tile), pl.ds(tile, frame)
    first, after = pl.ds(0, frame), pl.ds(frame, tile - frame)
    parts = [pl.ds(j * frame, frame) for j in range(chunks)]
    around = Around()
    sends = Sends(send_sems, recv_sems)
    corner_no, side_no, below_no = 0, 1, 3
    top_no = below_no + chunks
    rim_no = top_no + chunks
    there, source = around.has_right, around.has_left
    sends.add(corner_no, grad.at[:, rim, rim], in_corner, around.right, there, source)
    for j, part in enumerate((first, after)):
        sends.add(
            side_no + j, grad.at[:, part, rim], in_right.at[:, part, :], around.right, there, source
        )
    for j, part in enumerate(parts):
        sends.add(
            below_no + j, low if j == 0 else grad.at[:, rim, part], in_below.at[:, :, part],
            around.down, around.has_down, around.has_up,
        )
        if extend:
            sends.add(
                top_no + j, high if j == 0 else grad.at[:, first, part], in_top.at[:, :, part],
                around.up, around.has_up, around.has_down,
            )
    if extend:
        for j, part in enumerate((first, after)):
            sends.add(
                rim_no + j, new.at[:, part, first], new.at[:, part, rim], around.left,
                around.has_left, around.has_right,
            )
        sends.add(
            rim_no + 2, new.at[:, rim, first], new.at[:, rim, rim], around.left,
            around.has_left & around.has_down, around.has_right & around.has_down,
        )

    around.meet()

    def start_row(j):
        sends.start(below_no + j)
        if extend:
            sends.start(top_no + j)

    sends.start(corner_no)
    sends.start(side_no)
    if chunks > 1:
        start_row(1)
        sends.start(side_no + 1)

    @pl.when(jnp.logical_not(around.has_left))
    def _():
        in_right[...] = jnp.zeros_like(in_right)
        in_corner[...] = jnp.zeros_like(in_corner)

    @pl.when(jnp.logical_not(around.has_up))
    def _():
        in_below[...] = jnp.zeros_like(in_below)

    if extend:
        clear_edges(around, new, tile, frame)
    sends.arrived(corner_no)
    low[...] = grad[:, rim, first] + in_corner[...]
    sends.start(below_no)
    sends.arrived(side_no)
    if extend:
        high[...] = grad[:, first, first] + in_right[:, first, :]
        sends.start(top_no)
    for j in range(2, chunks):
        start_row(j)
    new[:, after, after] = ext[:, after, after] - step_size * grad[:, after, after]
    if chunks > 1:
        sends.arrived(side_no + 1)
        new[:, after, first] = ext[:, after, first] - step_size * (
            grad[:, after, first] + in_right[:, after, :]
        )
        if extend:
            sends.start(rim_no + 1)
    order = [1, 0] + list(range(2, chunks)) if chunks > 1 else [0]
    for j in order:
        part = parts[j]
        sends.arrived(below_no + j)
        total = grad[:, first, part] + in_below[:, :, part]
        if j == 0:
            total = total + in_right[:, first, :]
        new[:, first, part] = ext[:, first, part] - step_size * total
        if extend:
            if j == 0:
                sends.start(rim_no)
            sends.arrived(top_no + j)

            @pl.when(around.has_down)
            def _():
                own = low[...] if j == 0 else grad[:, rim, part]
                new[:, rim, part] = ext[:, rim, part] - step_size * (own + in_top[:, :, part])

            if j == 0:
                sends.start(rim_no + 2)
    if extend:
        for number in range(rim_no, rim_no + 3):
            if chunks > 1 or number != rim_no + 1:
                sends.arrived(number)
    sends.drain()


def extend_call(main, phase, later):
    tile, frame = main.shape[2], phase.shape[0]
    outside = pl.BlockSpec(memory_space=pltpu.HBM)
    vmem = pl.BlockSpec(memory_space=pltpu.VMEM)
    copies = tile // frame + 2
    whole = tile + frame
    return pl.pallas_call(
        functools.partial(extend_kernel, len(later)),
        out_shape=[
            jax.ShapeDtypeStruct((4, whole, whole), jnp.float32),
            jax.ShapeDtypeStruct((2, frame, frame), jnp.float32),
        ]
        + [jax.ShapeDtypeStruct(x.shape, x.dtype) for x in later],
        in_specs=[outside] * (2 + len(later)),
        out_specs=[vmem] * (2 + len(later)),
        scratch_shapes=[
            pltpu.VMEM(phase.shape, jnp.float32),
            pltpu.SemaphoreType.DMA((copies,)),
            pltpu.SemaphoreType.DMA((copies,)),
            pltpu.SemaphoreType.DMA((2 + len(later),)),
        ],
        compiler_params=pltpu.CompilerParams(
            collective_id=0, has_side_effects=True, vmem_limit_bytes=16 << 20
        ),
    )(*[pltpu.with_memory_space_constraint(x, pltpu.HBM) for x in (main, phase, *later)])


def fold_call(ext, grad, frame, extend):
    whole = ext.shape[2]
    tile = whole - frame
    vmem = pl.BlockSpec(memory_space=pltpu.VMEM)
    copies = 2 * (tile // frame) + 6
    side = whole if extend else tile
    block = pltpu.VMEM((4, frame, frame), jnp.float32)
    strip = pltpu.VMEM((4, frame, tile), jnp.float32)
    return pl.pallas_call(
        functools.partial(fold_kernel, extend, tile, frame),
        out_shape=jax.ShapeDtypeStruct((4, side, side), jnp.float32),
        in_specs=[vmem] * 2,
        out_specs=vmem,
        scratch_shapes=([strip, block] if extend else [])
        + [
            block,
            pltpu.VMEM((4, tile, frame), jnp.float32),
            strip,
            block,
            pltpu.SemaphoreType.DMA((copies,)),
            pltpu.SemaphoreType.DMA((copies,)),
        ],
        compiler_params=pltpu.CompilerParams(
            collective_id=1 if extend else 2, has_side_effects=True, vmem_limit_bytes=32 << 20
        ),
    )(ext, grad)


def local(object_tiles, probe_field, prop_phase, intensity, positions, counts):
    tile = object_tiles.shape[3]
    frame = probe_field.shape[1]
    tables = [jnp.asarray(t) for t in dft_tables(frame)]
    later = (counts, positions, probe_field, intensity, *tables)
    ext, kern, *near = extend_call(object_tiles.reshape(4, tile, tile), prop_phase, later)
    counts, positions, probe, measured, *tables = near
    for iteration in range(ITERS):
        grad = frame_grads(counts, positions, ext, probe, kern, measured, tables)
        ext = fold_call(ext, grad, frame, iteration < ITERS - 1)
    return ext.reshape(object_tiles.shape)


def solution(mesh):
    return jax.shard_map(
        local,
        mesh=mesh,
        in_specs=(
            P(None, None, "row", "col"),
            P(),
            P(),
            P(("row", "col"), None, None),
            P(("row", "col"), None),
            P("row", None),
        ),
        out_specs=P(None, None, "row", "col"),
        check_vma=False,
    )
```

```python
import functools

import jax
import jax.numpy as jnp
import numpy as np
from jax import lax
from jax.experimental import pallas as pl
from jax.experimental.pallas import tpu as pltpu
from jax.sharding import PartitionSpec as P

ITERS = 2
GROUP = 8
CHAIN = 2
SUB = 8

step_size = 0.2


def dft_tables(size):
    index = np.arange(size)
    phase = (index[:, None] * index[None, :] % size) * (2.0 * np.pi / size)
    re = np.cos(phase) / np.sqrt(size)
    im = -np.sin(phase) / np.sqrt(size)
    rights, lefts = [], []
    for sign in (1.0, -1.0):
        right = np.block([[re, sign * im], [-sign * im, re]]).astype(np.float32)
        high = right.astype(jnp.bfloat16)
        low = (right - high.astype(np.float32)).astype(jnp.bfloat16)
        rights.append(np.concatenate([high, high, low], axis=0))
        lefts.append(np.concatenate([high.T, high.T, low.T], axis=1))
    return np.stack(rights), np.stack(lefts)


def split(x):
    high = x.astype(jnp.bfloat16)
    low = (x - high.astype(jnp.float32)).astype(jnp.bfloat16)
    return high, low


def in_chains(transform):
    def over_all(waves, table):
        out = []
        for i in range(0, len(waves), CHAIN):
            out += transform(waves[i : i + CHAIN], table)
        return out

    return over_all


@in_chains
def by_right(waves, table):
    size = waves[0][0].shape[0]
    x = jnp.concatenate([jnp.concatenate(wave, axis=1) for wave in waves], axis=0)
    high, low = split(x)
    y = jnp.dot(
        jnp.concatenate([high, low, high], axis=1), table, preferred_element_type=jnp.float32
    )
    return [
        (y[i * size : (i + 1) * size, :size], y[i * size : (i + 1) * size, size:])
        for i in range(len(waves))
    ]


@in_chains
def by_left(waves, table):
    size = waves[0][0].shape[0]
    x = jnp.concatenate([jnp.concatenate(wave, axis=0) for wave in waves], axis=1)
    high, low = split(x)
    y = jnp.dot(
        table, jnp.concatenate([high, low, high], axis=0), preferred_element_type=jnp.float32
    )
    return [
        (y[:size, i * size : (i + 1) * size], y[size:, i * size : (i + 1) * size])
        for i in range(len(waves))
    ]


def mul(a, b):
    return (a[0] * b[0] - a[1] * b[1], a[0] * b[1] + a[1] * b[0])


def conj_mul(a, b):
    return (a[0] * b[0] + a[1] * b[1], a[0] * b[1] - a[1] * b[0])


def frames_kernel(
    counts_ref, pos_ref, ext, probe_ref, kern_ref, meas_ref, rtab_ref, ltab_ref, grad,
):
    frame = probe_ref.shape[1]
    slots = meas_ref.shape[0]
    grad[...] = jnp.zeros_like(grad)
    count = counts_ref[0, lax.axis_index("col")]
    lane = lax.broadcasted_iota(jnp.int32, (frame + SUB, frame), 1)
    sub = lax.broadcasted_iota(jnp.int32, (frame // SUB + 1, SUB, frame), 1)
    edge = jnp.zeros((1, SUB, frame), jnp.float32)

    @pl.loop(0, (count + GROUP - 1) // GROUP)
    def _(group):
        places, firsts, seconds = [], [], []
        for i in range(GROUP):
            slot = group * GROUP + i
            here = jnp.minimum(slot, slots - 1)
            weight = (slot < count).astype(jnp.float32)
            top = pos_ref[0, here]
            left = pos_ref[1, here]
            block = left // frame
            shift = left - block * frame
            near = pl.ds(pl.multiple_of(block * frame, frame), frame)
            far = pl.ds(pl.multiple_of(block * frame + frame, frame), frame)
            start = top // SUB * SUB
            drop = top - start
            rows = pl.ds(pl.multiple_of(start, SUB), frame + SUB)
            back = lax.rem(frame - shift, frame)
            lift = lax.rem(SUB - drop, SUB)
            planes = []
            for s in range(4):
                a = pltpu.roll(ext[s, rows, near], back, 1)
                b = pltpu.roll(ext[s, rows, far], back, 1)
                wide = jnp.where(lane < frame - shift, a, b).reshape(-1, SUB, frame)
                wide = pltpu.roll(wide, lift, 1)
                plane = jnp.where(sub[1:] < SUB - drop, wide[:-1], wide[1:])
                planes.append(plane.reshape(frame, frame))
            places.append((here, weight, rows, near, far, shift, drop))
            firsts.append((planes[0], planes[1]))
            seconds.append((planes[2], planes[3]))
        probe = (probe_ref[0], probe_ref[1])
        kern = (kern_ref[0], kern_ref[1])
        lit = [mul(probe, first) for first in firsts]
        freq = by_left(by_right(lit, rtab_ref[0]), ltab_ref[0])
        moved = [mul(kern, f) for f in freq]
        inner = by_right(by_left(moved, ltab_ref[1]), rtab_ref[1])
        leave = [mul(b, o) for b, o in zip(inner, seconds)]
        far_field = by_left(by_right(leave, rtab_ref[0]), ltab_ref[0])
        missed = []
        for place, (re, im) in zip(places, far_field):
            misfit = re * re + im * im - meas_ref[place[0]]
            missed.append((misfit * re, misfit * im))
        back_wave = by_right(by_left(missed, ltab_ref[1]), rtab_ref[1])
        grad_two = [conj_mul(b, g) for b, g in zip(inner, back_wave)]
        carry = [conj_mul(o, g) for o, g in zip(seconds, back_wave)]
        carried = by_left(by_right(carry, rtab_ref[0]), ltab_ref[0])
        unmoved = [conj_mul(kern, f) for f in carried]
        near_wave = by_right(by_left(unmoved, ltab_ref[1]), rtab_ref[1])
        grad_one = [conj_mul(probe, w) for w in near_wave]
        for place, one, two in zip(places, grad_one, grad_two):
            here, weight, rows, near, far, shift, drop = place
            for s, value in enumerate((one[0], one[1], two[0], two[1])):
                turned = pltpu.roll(value * weight, shift, 1).reshape(-1, SUB, frame)
                turned = pltpu.roll(turned, drop, 1)
                upper = jnp.concatenate([turned, edge], axis=0)
                lower = jnp.concatenate([edge, turned], axis=0)
                turned = jnp.where(sub >= drop, upper, lower).reshape(frame + SUB, frame)
                inside = lane >= shift
                grad[s, rows, near] += jnp.where(inside, turned, 0.0)
                grad[s, rows, far] += jnp.where(inside, 0.0, turned)


def frame_grads(counts, positions, ext, probe, kern, intensity, tables):
    smem = pl.BlockSpec(memory_space=pltpu.SMEM)
    vmem = pl.BlockSpec(memory_space=pltpu.VMEM)
    return pl.pallas_call(
        frames_kernel,
        out_shape=jax.ShapeDtypeStruct(ext.shape, jnp.float32),
        in_specs=[smem, smem] + [vmem] * 6,
        out_specs=vmem,
        compiler_params=pltpu.CompilerParams(vmem_limit_bytes=40 << 20),
    )(counts, positions, ext, probe, kern, intensity, *tables)


MESH = pl.DeviceIdType.MESH


class Around:
    def __init__(self):
        rows, cols = lax.axis_size("row"), lax.axis_size("col")
        row, col = lax.axis_index("row"), lax.axis_index("col")
        self.up = (lax.rem(row + rows - 1, rows), col)
        self.down = (lax.rem(row + 1, rows), col)
        self.left = (row, lax.rem(col + cols - 1, cols))
        self.right = (row, lax.rem(col + 1, cols))
        self.has_up = row > 0
        self.has_down = row < rows - 1
        self.has_left = col > 0
        self.has_right = col < cols - 1

    def meet(self):
        barrier = pltpu.get_barrier_semaphore()
        sides = (
            (self.has_up, self.up),
            (self.has_down, self.down),
            (self.has_left, self.left),
            (self.has_right, self.right),
        )
        for there, device in sides:

            @pl.when(there)
            def _():
                pl.semaphore_signal(barrier, inc=1, device_id=device, device_id_type=MESH)

        total = sum(there.astype(jnp.int32) for there, _ in sides)
        pl.semaphore_wait(barrier, total)


class Sends:
    def __init__(self, send_sems, recv_sems):
        self.send_sems, self.recv_sems = send_sems, recv_sems
        self.copies = {}

    def add(self, number, src, dst, device, has_target, has_source):
        copy = pltpu.make_async_remote_copy(
            src_ref=src,
            dst_ref=dst,
            send_sem=self.send_sems.at[number],
            recv_sem=self.recv_sems.at[number],
            device_id=device,
            device_id_type=MESH,
        )
        self.copies[number] = (copy, has_target, has_source)

    def start(self, number):
        copy, has_target, _ = self.copies[number]
        pl.when(has_target)(copy.start)

    def arrived(self, number):
        copy, _, has_source = self.copies[number]
        pl.when(has_source)(copy.wait_recv)

    def drain(self):
        for copy, has_target, _ in self.copies.values():
            pl.when(has_target)(copy.wait_send)


def extend_kernel(held, main, phase_hbm, *rest):
    later, (ext, kern), near = rest[:held], rest[held : held + 2], rest[held + 2 : 2 * held + 2]
    phase, send_sems, recv_sems, sems = rest[2 * held + 2 :]
    tile = main.shape[2]
    frame = phase.shape[0]
    chunks = tile // frame
    core, rim, first = pl.ds(0, tile), pl.ds(tile, frame), pl.ds(0, frame)
    around = Around()
    sends = Sends(send_sems, recv_sems)
    for j in range(chunks):
        part = pl.ds(j * frame, frame)
        sends.add(
            j, main.at[:, first, part], ext.at[:, rim, part], around.up,
            around.has_up, around.has_down,
        )
    sends.add(
        chunks, main.at[:, :, first], ext.at[:, core, rim], around.left,
        around.has_left, around.has_right,
    )
    sends.add(
        chunks + 1, ext.at[:, rim, first], ext.at[:, rim, rim], around.left,
        around.has_left & around.has_down, around.has_right & around.has_down,
    )
    around.meet()
    for number in range(chunks + 1):
        sends.start(number)
    phase_load = pltpu.make_async_copy(phase_hbm, phase, sems.at[0])
    loads = [pltpu.make_async_copy(main, ext.at[:, core, core], sems.at[1])] + [
        pltpu.make_async_copy(src, dst, sems.at[2 + i]) for i, (src, dst) in enumerate(zip(later, near))
    ]
    phase_load.start()
    for load in loads:
        load.start()
    phase_load.wait()
    kern[0] = jnp.cos(phase[...])
    kern[1] = jnp.sin(phase[...])
    clear_edges(around, ext, tile, frame)
    sends.arrived(0)
    sends.start(chunks + 1)
    for load in loads:
        load.wait()
    for number in range(1, chunks + 2):
        sends.arrived(number)
    sends.drain()


def clear_edges(around, ext, tile, frame):
    @pl.when(jnp.logical_not(around.has_right))
    def _():
        ext[:, :tile, tile:] = jnp.zeros((4, tile, frame), jnp.float32)

    @pl.when(jnp.logical_not(around.has_down))
    def _():
        ext[:, tile:, :tile] = jnp.zeros((4, frame, tile), jnp.float32)

    @pl.when(jnp.logical_not(around.has_right & around.has_down))
    def _():
        ext[:, tile:, tile:] = jnp.zeros((4, frame, frame), jnp.float32)


def fold_kernel(extend, tile, frame, ext, grad, new, *rest):
    if extend:
        in_top, high, *rest = rest
    low, in_right, in_below, in_corner, send_sems, recv_sems = rest
    chunks = tile // frame
    core, rim = pl.ds(0, tile), pl.ds(tile, frame)
    first, after = pl.ds(0, frame), pl.ds(frame, tile - frame)
    parts = [pl.ds(j * frame, frame) for j in range(chunks)]
    around = Around()
    sends = Sends(send_sems, recv_sems)
    corner_no, side_no, below_no = 0, 1, 3
    top_no = below_no + chunks
    rim_no = top_no + chunks
    there, source = around.has_right, around.has_left
    sends.add(corner_no, grad.at[:, rim, rim], in_corner, around.right, there, source)
    for j, part in enumerate((first, after)):
        sends.add(
            side_no + j, grad.at[:, part, rim], in_right.at[:, part, :], around.right, there, source
        )
    for j, part in enumerate(parts):
        sends.add(
            below_no + j, low if j == 0 else grad.at[:, rim, part], in_below.at[:, :, part],
            around.down, around.has_down, around.has_up,
        )
        if extend:
            sends.add(
                top_no + j, high if j == 0 else grad.at[:, first, part], in_top.at[:, :, part],
                around.up, around.has_up, around.has_down,
            )
    if extend:
        for j, part in enumerate((first, after)):
            sends.add(
                rim_no + j, new.at[:, part, first], new.at[:, part, rim], around.left,
                around.has_left, around.has_right,
            )
        sends.add(
            rim_no + 2, new.at[:, rim, first], new.at[:, rim, rim], around.left,
            around.has_left & around.has_down, around.has_right & around.has_down,
        )

    around.meet()

    def start_row(j):
        sends.start(below_no + j)
        if extend:
            sends.start(top_no + j)

    sends.start(corner_no)
    sends.start(side_no)
    if chunks > 1:
        start_row(1)
        sends.start(side_no + 1)

    @pl.when(jnp.logical_not(around.has_left))
    def _():
        in_right[...] = jnp.zeros_like(in_right)
        in_corner[...] = jnp.zeros_like(in_corner)

    @pl.when(jnp.logical_not(around.has_up))
    def _():
        in_below[...] = jnp.zeros_like(in_below)

    if extend:
        clear_edges(around, new, tile, frame)
    sends.arrived(corner_no)
    low[...] = grad[:, rim, first] + in_corner[...]
    sends.start(below_no)
    sends.arrived(side_no)
    if extend:
        high[...] = grad[:, first, first] + in_right[:, first, :]
        sends.start(top_no)
    for j in range(2, chunks):
        start_row(j)
    new[:, after, after] = ext[:, after, after] - step_size * grad[:, after, after]
    if chunks > 1:
        sends.arrived(side_no + 1)
        new[:, after, first] = ext[:, after, first] - step_size * (
            grad[:, after, first] + in_right[:, after, :]
        )
        if extend:
            sends.start(rim_no + 1)
    order = [1, 0] + list(range(2, chunks)) if chunks > 1 else [0]
    for j in order:
        part = parts[j]
        sends.arrived(below_no + j)
        total = grad[:, first, part] + in_below[:, :, part]
        if j == 0:
            total = total + in_right[:, first, :]
        new[:, first, part] = ext[:, first, part] - step_size * total
        if extend:
            if j == 0:
                sends.start(rim_no)
            sends.arrived(top_no + j)

            @pl.when(around.has_down)
            def _():
                own = low[...] if j == 0 else grad[:, rim, part]
                new[:, rim, part] = ext[:, rim, part] - step_size * (own + in_top[:, :, part])

            if j == 0:
                sends.start(rim_no + 2)
    if extend:
        for number in range(rim_no, rim_no + 3):
            if chunks > 1 or number != rim_no + 1:
                sends.arrived(number)
    sends.drain()


def extend_call(main, phase, later):
    tile, frame = main.shape[2], phase.shape[0]
    outside = pl.BlockSpec(memory_space=pltpu.HBM)
    vmem = pl.BlockSpec(memory_space=pltpu.VMEM)
    copies = tile // frame + 2
    whole = tile + frame
    return pl.pallas_call(
        functools.partial(extend_kernel, len(later)),
        out_shape=[
            jax.ShapeDtypeStruct((4, whole, whole), jnp.float32),
            jax.ShapeDtypeStruct((2, frame, frame), jnp.float32),
        ]
        + [jax.ShapeDtypeStruct(x.shape, x.dtype) for x in later],
        in_specs=[outside] * (2 + len(later)),
        out_specs=[vmem] * (2 + len(later)),
        scratch_shapes=[
            pltpu.VMEM(phase.shape, jnp.float32),
            pltpu.SemaphoreType.DMA((copies,)),
            pltpu.SemaphoreType.DMA((copies,)),
            pltpu.SemaphoreType.DMA((2 + len(later),)),
        ],
        compiler_params=pltpu.CompilerParams(
            collective_id=0, has_side_effects=True, vmem_limit_bytes=16 << 20
        ),
    )(*[pltpu.with_memory_space_constraint(x, pltpu.HBM) for x in (main, phase, *later)])


def fold_call(ext, grad, frame, extend):
    whole = ext.shape[2]
    tile = whole - frame
    vmem = pl.BlockSpec(memory_space=pltpu.VMEM)
    copies = 2 * (tile // frame) + 6
    side = whole if extend else tile
    block = pltpu.VMEM((4, frame, frame), jnp.float32)
    strip = pltpu.VMEM((4, frame, tile), jnp.float32)
    return pl.pallas_call(
        functools.partial(fold_kernel, extend, tile, frame),
        out_shape=jax.ShapeDtypeStruct((4, side, side), jnp.float32),
        in_specs=[vmem] * 2,
        out_specs=vmem,
        scratch_shapes=([strip, block] if extend else [])
        + [
            block,
            pltpu.VMEM((4, tile, frame), jnp.float32),
            strip,
            block,
            pltpu.SemaphoreType.DMA((copies,)),
            pltpu.SemaphoreType.DMA((copies,)),
        ],
        compiler_params=pltpu.CompilerParams(
            collective_id=1 if extend else 2, has_side_effects=True, vmem_limit_bytes=32 << 20
        ),
    )(ext, grad)


def local(object_tiles, probe_field, prop_phase, intensity, positions, counts):
    tile = object_tiles.shape[3]
    frame = probe_field.shape[1]
    tables = [jnp.asarray(t) for t in dft_tables(frame)]
    later = (counts, positions.T, probe_field, intensity, *tables)
    ext, kern, *near = extend_call(object_tiles.reshape(4, tile, tile), prop_phase, later)
    counts, positions, probe, measured, *tables = near
    for iteration in range(ITERS):
        grad = frame_grads(counts, positions, ext, probe, kern, measured, tables)
        ext = fold_call(ext, grad, frame, iteration < ITERS - 1)
    return ext.reshape(object_tiles.shape)


def solution(mesh):
    return jax.shard_map(
        local,
        mesh=mesh,
        in_specs=(
            P(None, None, "row", "col"),
            P(),
            P(),
            P(("row", "col"), None, None),
            P(("row", "col"), None),
            P("row", None),
        ),
        out_specs=P(None, None, "row", "col"),
        check_vma=False,
    )
```
